32 devices in a mesh: groups: 2 (over y), seq: 4 (over z), head: 2 (over x), cfg: 2 (over core).
Axes of the slice: x: 2, y: 2, z: 4, core: 2. Of those that a mesh axis runs over, the one named last changes fastest.
Arguments:
- queries: bfloat16 [2, 1024, 3072], P('cfg', ('groups', 'seq'), 'head'), parts along dimension 1, may hold values from -60 to 60
- keys: bfloat16 [2, 1024, 3072], P('cfg', ('groups', 'seq'), 'head'), parts along dimension 1, may hold values from -3 to 3
- values: bfloat16 [2, 1024, 3072], P('cfg', ('groups', 'seq'), 'head'), parts along dimension 1, may hold values from -6 to 6
- band_mask: int32 [48, 4, 4], P(('groups', 'head')), parts along dimension 0, may hold values from 0 to 1, as said below
- out_weight: bfloat16 [3072, 3072], P('head', 'cfg'), may hold values from -0.109375 to 0.109375
- guidance: float32 [1], replicated, may hold values from 3 to 8
Outputs:
- projected: bfloat16 [1024, 3072], P(('groups', 'seq'), ('cfg', 'head')), parts along dimension 0
The draws below stay inside these ranges and needn't reach their ends.
There are 2 independent parts, one for each index of `groups`. The reference program is written for one: setup_inputs(seed, part) draws one part's arguments, and reference() takes and returns one part's arrays. A program takes and returns all parts, laid end to end along the dimension named above; an argument that names none is the same for every part. Nothing has to cross between parts.
Inputs may be any that keep to these rules, and one draw needn't show every extreme that they name: `band_mask`: densities are drawn per head.
All inputs are finite; a program needn't handle non-finite values.
Results may differ from the reference program's by a relative error of at most 0.02.
Values may be sent and summed in bfloat16 or wider, within the bound.
A program may use at most 128 MiB of HBM per device.

```python
import jax
import jax.numpy as jnp
from jax import lax

D = 3072
HD = 128
HEADS = 24
Q_DEV = 128
KV_DEV = 128
TILES = 4
QUERIES = 512
KEYS = 512


def shared_keys(key):
    base = jax.random.fold_in(key, 7)
    keyset = jnp.clip(jax.random.normal(base, (2, KEYS, HEADS * HD), jnp.float32), -3.0, 3.0)
    return keyset


def draw_keys(key, part):
    return shared_keys(key).astype(jnp.bfloat16)


def draw_queries(key, part):
    querset = jnp.clip(jax.random.normal(jax.random.fold_in(key, 11), (2, QUERIES, HEADS * HD), jnp.float32), -6.0, 6.0)
    return querset.astype(jnp.bfloat16)


def draw_band_mask(key, part):
    density = jax.random.randint(jax.random.fold_in(key, 21), (HEADS, 1, 1), 1, 8)
    levels = jax.random.randint(jax.random.fold_in(key, 22), (HEADS, TILES, TILES), 0, 8)
    return (levels < density).astype(jnp.int32)


def level_of(key, extent, shards, least, top_value):
    factor_of = 1.0
    for axis_at, shards_of in shards:
        heights = jax.random.uniform(jax.random.fold_in(jax.random.fold_in(key, 6), axis_at), (shards_of,), jnp.float32, least / len(shards), top_value / len(shards))
        factor_of = factor_of * jnp.repeat(jnp.exp(heights), extent[axis_at] // shards_of).reshape((-1,) + (1,) * (len(extent) - 1 - axis_at))
    return factor_of


def bell_draw(key, shape, spread, reach, cuts=(), held_as=jnp.bfloat16):
    entries = jax.random.normal(key, shape, jnp.float32) * spread
    if len(cuts) > 0:
        entries = level_of(key, shape, cuts, -0.22, 0.18) * entries
    return jnp.clip(entries, min=-reach, max=reach).astype(held_as)


def setup_inputs(seed: int = 0, part: int = 0) -> dict:
    splits = jax.random.split(jax.random.key(seed), 7)
    part_keys = jax.random.split(jax.random.fold_in(splits[6], part), 7)
    return {
        "queries": draw_queries(jax.random.fold_in(jax.random.fold_in(splits[6], part), 71), part),
        "keys": draw_keys(jax.random.fold_in(jax.random.fold_in(splits[6], part), 71), part),
        "values": bell_draw(part_keys[2], (2, KEYS, HEADS * HD), 1.0, 6.0, ((0, 2), (1, 4), (2, 2))),
        "band_mask": draw_band_mask(jax.random.fold_in(jax.random.fold_in(splits[6], part), 71), part),
        "out_weight": bell_draw(splits[4], (HEADS * HD, D), (HEADS * HD) ** -0.5, 0.109375, ((0, 2), (1, 2))),
        "guidance": jnp.clip(jax.random.uniform(splits[5], (1,), jnp.float32, 3.0, 8.0), 3.0, 8.0),
    }


def reference(queries, keys, values, band_mask, out_weight, guidance):
    scale = HD ** -0.5
    tile_of_q = (jnp.arange(QUERIES) // Q_DEV).astype(jnp.int32)
    band_of_k = (jnp.arange(KEYS) // KV_DEV).astype(jnp.int32)
    ident = jnp.eye(TILES, dtype=jnp.int32)
    qh = jnp.transpose(queries.reshape(2, QUERIES, HEADS, HD), (2, 0, 1, 3))
    kh = jnp.transpose(keys.reshape(2, KEYS, HEADS, HD), (2, 0, 1, 3))
    vh = jnp.transpose(values.reshape(2, KEYS, HEADS, HD), (2, 0, 1, 3))

    def one_head(args):
        qq, kk, vv, mask = args
        allowed = (mask + ident) > 0
        full = allowed[tile_of_q][:, band_of_k]
        outs = []
        for copy in range(2):
            scores = jnp.dot(qq[copy], kk[copy].T, preferred_element_type=jnp.float32) * scale
            scores = jnp.where(full, scores, -1e30)
            top = jnp.max(scores, axis=1, keepdims=True)
            expo = jnp.where(full, jnp.exp(scores - top), 0.0)
            total = jnp.sum(expo, axis=1, keepdims=True)
            outs.append(jnp.dot(expo.astype(jnp.bfloat16), vv[copy], preferred_element_type=jnp.float32) / total)
        return jnp.stack(outs).astype(jnp.bfloat16)

    attn = lax.map(one_head, (qh, kh, vh, band_mask))
    attn = jnp.transpose(attn, (1, 2, 0, 3)).reshape(2, QUERIES, HEADS * HD)
    cond = attn[0].astype(jnp.float32)
    uncond = attn[1].astype(jnp.float32)
    guided = (uncond + guidance[0] * (cond - uncond)).astype(jnp.bfloat16)
    return jnp.dot(guided, out_weight, preferred_element_type=jnp.float32).astype(jnp.bfloat16)
```

```python
import functools

import jax
import jax.numpy as jnp
from jax import lax
from jax.experimental import pallas as pl
from jax.experimental.pallas import tpu as pltpu
from jax.sharding import PartitionSpec as P

HD = 128
MESH = pl.DeviceIdType.MESH
LOG2E = 1.4426950408889634


def flipped(index, bits):
    out = index
    bit = 1
    while bit <= bits:
        if bits // bit % 2:
            out = out + bit - 2 * bit * lax.rem(lax.div(index, bit), 2)
        bit *= 2
    return out


def remote(src, dst, send, recv, device):
    copy = pltpu.make_async_remote_copy(
        src_ref=src, dst_ref=dst, send_sem=send, recv_sem=recv, device_id=device, device_id_type=MESH
    )
    copy.start()
    return copy


def kernel(
    n, hp, parts,
    q_ref, k_ref, v_ref, mask_ref, w_ref, g_ref, out_ref,
    q_buf, k_buf, v_buf, w_buf, att, other, guid, rows, acc, sends, recvs,
    load_sem, w_sem, a_send, a_recv, x_send, x_recv, r_send, r_recv, s_send, s_recv, h_send, h_recv,
):
    me = lax.axis_index("seq")
    core = lax.axis_index("cfg")
    side = lax.axis_index("head")
    T = q_ref.shape[1]
    half = T // 2
    cols = out_ref.shape[1]
    width = cols // len(range(0, cols, 256)) if cols % 256 == 0 else cols

    loads = []
    mine = pl.multiple_of(me * T, T)
    for i, (ref, buf) in enumerate(((q_ref, q_buf), (k_ref, k_buf), (v_ref, v_buf))):
        for j in range(hp):
            at = pl.multiple_of((me * hp + j) * HD, HD)
            c = pltpu.make_async_copy(ref.at[0, :, pl.ds(at, HD)], buf.at[j, pl.ds(mine, T), :], load_sem.at[j, i])
            c.start()
            loads.append(c)
    sibling = {"cfg": 1 - core}
    barrier = pltpu.get_barrier_semaphore()
    for k in range(1, n):
        pl.semaphore_signal(barrier, inc=1, device_id={"seq": flipped(me, k)}, device_id_type=MESH)
    pl.semaphore_signal(barrier, inc=1, device_id=sibling, device_id_type=MESH)
    for d in range(1, parts):
        pl.semaphore_signal(barrier, inc=1, device_id={"head": lax.rem(side + d, parts)}, device_id_type=MESH)
    pl.semaphore_wait(barrier, n - 1 + 1 + parts - 1)

    a2a = {}
    for j in range(hp):
        for k in range(n - 1, 0, -1):
            dest = flipped(me, k)
            at = pl.multiple_of((dest * hp + j) * HD, HD)
            for i, (ref, buf) in enumerate(((q_ref, q_buf), (k_ref, k_buf), (v_ref, v_buf))):
                a2a[j, k, i] = remote(
                    ref.at[0, :, pl.ds(at, HD)], buf.at[j, pl.ds(mine, T), :],
                    a_send.at[j, k - 1, i], a_recv.at[j, k - 1, i], {"seq": dest},
                )
    w_loads = []
    for j in range(hp):
        for z in range(n):
            c = pltpu.make_async_copy(
                w_ref.at[pl.ds((z * hp + j) * HD, HD), :], w_buf.at[j, pl.ds(z * HD, HD), :], w_sem.at[j, z]
            )
            c.start()
            w_loads.append(c)

    scale = HD ** (-0.5) * LOG2E
    guidance = g_ref[0]
    first = core == 0
    half_at = pl.multiple_of(core * half, half)
    pending = []
    backs = {}

    own_at = pl.multiple_of(me * HD, HD)
    siblings = {}
    for j in range(hp):
        for i in range(3):
            loads[i * hp + j].wait()
            for k in range(1, n):
                a2a[j, k, i].wait_recv()
        head = me * hp + j
        for t in range(n):
            q = q_buf[j, t * T:(t + 1) * T, :]
            s = lax.dot_general(q, k_buf[j], (((1,), (1,)), ((), ())), preferred_element_type=jnp.float32)
            pieces = []
            for b in range(n):
                listed = mask_ref[head, t, b] > 0
                bias = 0.0 if b == t else jnp.where(listed, 0.0, -1e30).astype(jnp.float32)
                pieces.append(s[:, b * T:(b + 1) * T] * scale + bias)
            s = jnp.concatenate(pieces, axis=1)
            top = jnp.max(s, axis=1, keepdims=True)
            expo = jnp.exp2(s - top)
            total = jnp.sum(expo, axis=1, keepdims=True)
            o = jnp.dot(expo.astype(jnp.bfloat16), v_buf[j], preferred_element_type=jnp.float32)
            o = (o * (1.0 / total)).astype(jnp.bfloat16)
            att[j, 0, t] = o[:half]
            att[j, 1, t] = o[half:]
        swap = remote(att.at[j, 1 - core], other.at[j], x_send.at[j], x_recv.at[j], sibling)
        swap.wait_recv()
        own = att[j, core].astype(jnp.float32)
        oth = other[j].astype(jnp.float32)
        cond = jnp.where(first, own, oth)
        uncond = jnp.where(first, oth, own)
        guid[j] = (uncond + guidance * (cond - uncond)).astype(jnp.bfloat16)
        for k in range(n - 1, 0, -1):
            dest = flipped(me, k)
            backs[j, k] = remote(
                guid.at[j, dest], rows.at[j, pl.ds(half_at, half), pl.ds(own_at, HD)],
                r_send.at[j, k - 1], r_recv.at[j, k - 1], {"seq": dest},
            )
        siblings[j] = [remote(
            guid.at[j, me], rows.at[j, pl.ds(half_at, half), pl.ds(own_at, HD)], s_send.at[j, 0], s_recv.at[j, 0], sibling
        )]
        rows[j, pl.ds(half_at, half), pl.ds(own_at, HD)] = guid[j, me]
        pending.append(swap)

        def forward(j):
            for k in range(1, n):
                backs[j, k].wait_recv()
                at = pl.multiple_of(flipped(me, k) * HD, HD)
                block = rows.at[j, pl.ds(half_at, half), pl.ds(at, HD)]
                siblings[j].append(remote(block, block, s_send.at[j, k], s_recv.at[j, k], sibling))

        if j > 0:
            forward(j - 1)
    forward(hp - 1)

    for c in w_loads:
        c.wait()
    for j in range(hp - 1):
        for copy in siblings[j]:
            copy.wait_recv()
        term = jnp.dot(rows[j], w_buf[j], preferred_element_type=jnp.float32)
        acc[...] = term if j == 0 else acc[...] + term
    j = hp - 1
    for copy in siblings[j]:
        copy.wait_recv()
    last = rows[j]
    outs = []
    for d in range(1, parts + 1):
        to = lax.rem(side + d, parts)
        for p in range(cols // width):
            at = pl.multiple_of(to * cols + p * width, width)
            term = jnp.dot(last, w_buf[j, :, pl.ds(at, width)], preferred_element_type=jnp.float32)
            if hp > 1:
                term = term + acc[:, pl.ds(at, width)]
            span = pl.ds(p * width, width)
            if d < parts:
                sends[d - 1, p] = term.astype(jnp.bfloat16)
                outs.append(remote(
                    sends.at[d - 1, p], recvs.at[d - 1, p], h_send.at[d - 1, p], h_recv.at[d - 1, p], {"head": to}
                ))
            else:
                acc[:, pl.ds(at, width)] = term
    for p in range(cols // width):
        at = pl.multiple_of(side * cols + p * width, width)
        total = acc[:, pl.ds(at, width)]
        for d in range(1, parts):
            outs[(d - 1) * (cols // width) + p].wait_recv()
            total = total + recvs[d - 1, p].astype(jnp.float32)
        out_ref[:, p * width:(p + 1) * width] = total.astype(jnp.bfloat16)
    for copy in list(a2a.values()) + pending + list(backs.values()) + sum(siblings.values(), []) + outs:
        copy.wait_send()


def by_heads(queries, keys, values, band_mask, out_weight, guidance):
    n = lax.axis_size("seq")
    parts = lax.axis_size("head")
    T, local = queries.shape[1], queries.shape[2]
    hp = local // HD // n
    wide = out_weight.shape[1]
    cols = wide // parts
    width = 256 if cols % 256 == 0 else cols
    half = T // 2
    bf, f32 = jnp.bfloat16, jnp.float32
    any_spec = pl.BlockSpec(memory_space=pl.ANY)
    smem = pl.BlockSpec(memory_space=pltpu.SMEM)
    dma = pltpu.SemaphoreType.DMA
    return pl.pallas_call(
        functools.partial(kernel, n, hp, parts),
        out_shape=jax.ShapeDtypeStruct((T, cols), bf),
        in_specs=[any_spec, any_spec, any_spec, smem, any_spec, smem],
        out_specs=pl.BlockSpec(memory_space=pltpu.VMEM),
        scratch_shapes=[
            pltpu.VMEM((hp, n * T, HD), bf),
            pltpu.VMEM((hp, n * T, HD), bf),
            pltpu.VMEM((hp, n * T, HD), bf),
            pltpu.VMEM((hp, n * HD, wide), bf),
            pltpu.VMEM((hp, 2, n, half, HD), bf),
            pltpu.VMEM((hp, n, half, HD), bf),
            pltpu.VMEM((hp, n, half, HD), bf),
            pltpu.VMEM((hp, T, n * HD), bf),
            pltpu.VMEM((T, wide), f32),
            pltpu.VMEM((parts - 1, cols // width, T, width), bf),
            pltpu.VMEM((parts - 1, cols // width, T, width), bf),
            dma((hp, 3)), dma((hp, n)),
            dma((hp, n - 1, 3)), dma((hp, n - 1, 3)),
            dma((hp,)), dma((hp,)),
            dma((hp, n - 1)), dma((hp, n - 1)),
            dma((hp, n)), dma((hp, n)),
            dma((parts - 1, cols // width)), dma((parts - 1, cols // width)),
        ],
        compiler_params=pltpu.CompilerParams(
            collective_id=0, has_side_effects=True, vmem_limit_bytes=60 * 1024 * 1024
        ),
        name="by_heads",
    )(queries, keys, values, band_mask, out_weight, guidance)


def swapped(array, axis, bit):
    return lax.ppermute(array, axis, [(i, i ^ 1 << bit) for i in range(lax.axis_size(axis))])


def by_rows(queries, keys, values, band_mask, out_weight, guidance):
    own_q = queries[0]
    own_k = keys[0]
    own_v = values[0]
    q_rows = own_q.shape[0]
    kv_rows = own_k.shape[0]
    local_heads = own_q.shape[1] // HD
    tiles = lax.axis_size("seq")
    place = lax.axis_index("seq")
    scale = HD ** (-0.5)
    bands = jnp.arange(tiles)
    ident = (bands[:, None] == bands[None, :]).astype(jnp.int32)
    allowed = band_mask + ident[None] > 0
    q_heads = own_q.reshape(q_rows, local_heads, HD)
    my_row = lax.dynamic_index_in_dim(allowed, place, 1, keepdims=False)
    k_piece = lax.all_gather(own_k, "seq", axis=0, tiled=True)
    v_piece = lax.all_gather(own_v, "seq", axis=0, tiled=True)
    count = k_piece.shape[0]
    band = jnp.arange(count) // kv_rows
    onehot = band[:, None] == bands[None, :]
    keymask = jnp.any(onehot[None] & my_row[:, None, :], axis=-1)
    top = jnp.full((local_heads, q_rows), -1e30, jnp.float32)
    k_heads = k_piece.reshape(count, local_heads, HD)
    v_heads = v_piece.reshape(count, local_heads, HD)
    scores = (
        jnp.einsum("qhd,khd->hqk", q_heads, k_heads, preferred_element_type=jnp.float32) * scale
    )
    scores = jnp.where(keymask[:, None, :], scores, -1e30)
    new_top = jnp.maximum(top, jnp.max(scores, axis=-1))
    expo = jnp.where(keymask[:, None, :], jnp.exp(scores - new_top[..., None]), 0.0)
    total = jnp.sum(expo, axis=-1)
    accum = jnp.einsum(
        "hqk,khd->hqd", expo.astype(jnp.bfloat16), v_heads, preferred_element_type=jnp.float32
    )
    top, total, accum = (new_top, total, accum)
    attn = accum / total[..., None]
    own_rows = jnp.transpose(attn, (1, 0, 2)).reshape(q_rows, local_heads * HD).astype(jnp.bfloat16)
    partner = swapped(own_rows, "cfg", 0)
    first_copy = lax.axis_index("cfg") == 0
    cond = jnp.where(first_copy, own_rows, partner).astype(jnp.float32)
    uncond = jnp.where(first_copy, partner, own_rows).astype(jnp.float32)
    guided = (uncond + guidance[0] * (cond - uncond)).astype(jnp.bfloat16)
    terms = jnp.dot(guided, out_weight, preferred_element_type=jnp.float32)
    return lax.psum_scatter(terms.astype(jnp.bfloat16), "head", scatter_dimension=1, tiled=True)


def shards(queries, *rest):
    seq = lax.axis_size("seq")
    heads = queries.shape[2] // HD
    if heads % seq == 0 and seq & (seq - 1) == 0 and lax.axis_size("cfg") == 2:
        return by_heads(queries, *rest)
    return by_rows(queries, *rest)


def solution(mesh):
    in_specs = (
        P("cfg", ("groups", "seq"), "head"),
        P("cfg", ("groups", "seq"), "head"),
        P("cfg", ("groups", "seq"), "head"),
        P(("groups", "head"), None, None),
        P("head", "cfg"),
        P(),
    )
    out_specs = P(("groups", "seq"), ("cfg", "head"))
    return jax.shard_map(shards, mesh=mesh, in_specs=in_specs, out_specs=out_specs, check_vma=False)
```

```python
import functools

import jax
import jax.numpy as jnp
from jax import lax
from jax.experimental import pallas as pl
from jax.experimental.pallas import tpu as pltpu
from jax.sharding import PartitionSpec as P

HD = 128
MESH = pl.DeviceIdType.MESH
LOG2E = 1.4426950408889634


def flipped(index, bits):
    out = index
    bit = 1
    while bit <= bits:
        if bits // bit % 2:
            out = out + bit - 2 * bit * lax.rem(lax.div(index, bit), 2)
        bit *= 2
    return out


def remote(src, dst, send, recv, device):
    copy = pltpu.make_async_remote_copy(
        src_ref=src, dst_ref=dst, send_sem=send, recv_sem=recv, device_id=device, device_id_type=MESH
    )
    copy.start()
    return copy


def kernel(
    n, hp, sets,
    q_ref, k_ref, v_ref, mask_ref, w_ref, g_ref, out_ref,
    q_buf, k_buf, v_buf, w_buf, att, other, guid, rows, acc,
    load_sem, w_sem, a_send, a_recv, x_send, x_recv, r_send, r_recv, f_send, f_recv,
    wx_send, wx_recv, wy_send, wy_recv,
):
    me = lax.axis_index("seq")
    core = lax.axis_index("cfg")
    side = lax.axis_index("head")
    group = lax.axis_index("groups")
    T = q_ref.shape[1]
    half = T // 2
    cols = out_ref.shape[1]
    share = n // sets
    tensors = ((q_ref, q_buf), (k_ref, k_buf), (v_ref, v_buf))
    sibling = {"cfg": 1 - core}
    across = {"head": 1 - side}
    facing = {"head": 1 - side, "cfg": 1 - core}
    groups = [{"groups": lax.rem(group + d, sets)} for d in range(1, sets)]

    barrier = pltpu.get_barrier_semaphore()
    for device in [{"seq": flipped(me, k)} for k in range(1, n)] + [sibling, across, facing] + groups:
        pl.semaphore_signal(barrier, inc=1, device_id=device, device_id_type=MESH)

    loads = {}
    mine = pl.multiple_of(me * T, T)
    for j in range(hp):
        at = pl.multiple_of((me * hp + j) * HD, HD)
        for i, (ref, buf) in enumerate(tensors):
            loads[j, i] = pltpu.make_async_copy(
                ref.at[0, :, pl.ds(at, HD)], buf.at[j, pl.ds(mine, T), :], load_sem.at[j, i]
            )
            loads[j, i].start()
    w_loads = {}
    own_cols = pl.ds(pl.multiple_of(side * cols, cols), cols)
    for j in range(hp):
        for z in range(n):
            w_loads[j, z] = pltpu.make_async_copy(
                w_ref.at[pl.ds((z * hp + j) * HD, HD), own_cols], w_buf.at[0, j, pl.ds(z * HD, HD), :], w_sem.at[j, z]
            )
    pl.semaphore_wait(barrier, n - 1 + 3 + sets - 1)

    a2a = {}
    across_w = {}
    their_cols = pl.ds(pl.multiple_of((1 - side) * cols, cols), cols)
    for j in range(hp):
        for k in range(n - 1, 0, -1):
            dest = flipped(me, k)
            at = pl.multiple_of((dest * hp + j) * HD, HD)
            for i, (ref, buf) in enumerate(tensors):
                a2a[j, k, i] = remote(
                    ref.at[0, :, pl.ds(at, HD)], buf.at[j, pl.ds(mine, T), :],
                    a_send.at[j, k - 1, i], a_recv.at[j, k - 1, i], {"seq": dest},
                )
        for i in range(share):
            z = group * share + i
            at = pl.multiple_of((z * hp + j) * HD, HD)
            across_w[j, i] = remote(
                w_ref.at[pl.ds(at, HD), their_cols],
                w_buf.at[1, j, pl.ds(pl.multiple_of(z * HD, HD), HD), :],
                wx_send.at[j, i], wx_recv.at[j, i], across,
            )
    for copy in w_loads.values():
        copy.start()

    scale = HD ** (-0.5) * LOG2E
    guidance = g_ref[0]
    first = core == 0
    my_half = pl.ds(pl.multiple_of(core * half, half), half)
    swaps, backs, relays, group_w = {}, {}, {}, {}

    def pass_on(j, src, block, z, at):
        for i, (slot, device) in enumerate(((0, sibling), (1, across), (1, facing))):
            relays[j, src, i] = remote(
                block, rows.at[slot, j, my_half, pl.ds(at, HD)], f_send.at[i, j, src], f_recv.at[i, j, src], device
            )

    for j in range(hp):
        for i in range(share):
            across_w[j, i].wait_recv()
            z = group * share + i
            block = w_buf.at[1, j, pl.ds(pl.multiple_of(z * HD, HD), HD), :]
            for d, device in enumerate(groups):
                group_w[d, j, i] = remote(block, block, wy_send.at[d, j, i], wy_recv.at[d, j, i], device)
        for i in range(3):
            loads[j, i].wait()
            for k in range(1, n):
                a2a[j, k, i].wait_recv()
        head = me * hp + j
        for t in range(n):
            q = q_buf[j, t * T:(t + 1) * T, :]
            s = lax.dot_general(q, k_buf[j], (((1,), (1,)), ((), ())), preferred_element_type=jnp.float32)
            pieces = []
            for b in range(n):
                piece = s[:, b * T:(b + 1) * T] * scale
                if b != t:
                    piece = piece + jnp.where(mask_ref[t, b, head] > 0, 0.0, -1e30).astype(jnp.float32)
                pieces.append(piece)
            s = jnp.concatenate(pieces, axis=1)
            top = jnp.max(s, axis=1, keepdims=True)
            expo = jnp.exp2(s - top)
            total = jnp.sum(expo, axis=1, keepdims=True)
            o = jnp.dot(expo.astype(jnp.bfloat16), v_buf[j], preferred_element_type=jnp.float32)
            o = (o * (1.0 / total)).astype(jnp.bfloat16)
            att[j, 0, t] = o[:half]
            att[j, 1, t] = o[half:]
        swaps[j] = remote(att.at[j, 1 - core], other.at[j], x_send.at[j], x_recv.at[j], sibling)
        swaps[j].wait_recv()
        own = att[j, core].astype(jnp.float32)
        oth = other[j].astype(jnp.float32)
        cond = jnp.where(first, own, oth)
        uncond = jnp.where(first, oth, own)
        guid[j] = (uncond + guidance * (cond - uncond)).astype(jnp.bfloat16)
        own_at = pl.multiple_of(me * HD, HD)
        for k in range(n - 1, 0, -1):
            dest = flipped(me, k)
            backs[j, k] = remote(
                guid.at[j, dest], rows.at[0, j, my_half, pl.ds(own_at, HD)],
                r_send.at[j, k - 1], r_recv.at[j, k - 1], {"seq": dest},
            )
        pass_on(j, 0, guid.at[j, me], me, own_at)
        rows[0, j, my_half, pl.ds(own_at, HD)] = guid[j, me]

    for j in range(hp):
        for k in range(1, n):
            backs[j, k].wait_recv()
            z = flipped(me, k)
            at = pl.multiple_of(z * HD, HD)
            pass_on(j, k, rows.at[0, j, my_half, pl.ds(at, HD)], z, at)

    for copy in w_loads.values():
        copy.wait()
    for copy in group_w.values():
        copy.wait_recv()
    for j in range(hp):
        for slot, kinds in ((0, (0,)), (1, (1, 2))):
            for k in range(n):
                for i in kinds:
                    relays[j, k, i].wait_recv()
            term = jnp.dot(rows[slot, j], w_buf[slot, j], preferred_element_type=jnp.float32)
            if j + slot > 0:
                term = acc[...] + term
            if slot == 1 and j == hp - 1:
                out_ref[...] = term.astype(jnp.bfloat16)
            else:
                acc[...] = term
    for copies in (a2a, across_w, swaps, backs, relays, group_w):
        for copy in copies.values():
            copy.wait_send()


def by_heads(queries, keys, values, band_mask, out_weight, guidance):
    n = lax.axis_size("seq")
    sides = lax.axis_size("head")
    sets = lax.axis_size("groups")
    T, local = queries.shape[1], queries.shape[2]
    hp = local // HD // n
    cols = out_weight.shape[1] // sides
    half = T // 2
    share = n // sets
    bf = jnp.bfloat16
    any_spec = pl.BlockSpec(memory_space=pl.ANY)
    smem = pl.BlockSpec(memory_space=pltpu.SMEM)
    dma = pltpu.SemaphoreType.DMA
    return pl.pallas_call(
        functools.partial(kernel, n, hp, sets),
        out_shape=jax.ShapeDtypeStruct((T, cols), bf),
        in_specs=[any_spec, any_spec, any_spec, smem, any_spec, smem],
        out_specs=pl.BlockSpec(memory_space=pltpu.VMEM),
        scratch_shapes=[
            pltpu.VMEM((hp, n * T, HD), bf),
            pltpu.VMEM((hp, n * T, HD), bf),
            pltpu.VMEM((hp, n * T, HD), bf),
            pltpu.VMEM((sides, hp, n * HD, cols), bf),
            pltpu.VMEM((hp, 2, n, half, HD), bf),
            pltpu.VMEM((hp, n, half, HD), bf),
            pltpu.VMEM((hp, n, half, HD), bf),
            pltpu.VMEM((sides, hp, T, n * HD), bf),
            pltpu.VMEM((T, cols), jnp.float32),
            dma((hp, 3)), dma((hp, n)),
            dma((hp, n - 1, 3)), dma((hp, n - 1, 3)),
            dma((hp,)), dma((hp,)),
            dma((hp, n - 1)), dma((hp, n - 1)),
            dma((3, hp, n)), dma((3, hp, n)),
            dma((hp, share)), dma((hp, share)),
            dma((sets - 1, hp, share)), dma((sets - 1, hp, share)),
        ],
        compiler_params=pltpu.CompilerParams(
            collective_id=0, has_side_effects=True, vmem_limit_bytes=60 * 1024 * 1024
        ),
        name="by_heads",
    )(queries, keys, values, jnp.transpose(band_mask, (1, 2, 0)), out_weight, guidance)


def swapped(array, axis, bit):
    return lax.ppermute(array, axis, [(i, i ^ 1 << bit) for i in range(lax.axis_size(axis))])


def by_rows(queries, keys, values, band_mask, out_weight, guidance):
    own_q = queries[0]
    own_k = keys[0]
    own_v = values[0]
    q_rows = own_q.shape[0]
    kv_rows = own_k.shape[0]
    local_heads = own_q.shape[1] // HD
    tiles = lax.axis_size("seq")
    place = lax.axis_index("seq")
    scale = HD ** (-0.5)
    bands = jnp.arange(tiles)
    ident = (bands[:, None] == bands[None, :]).astype(jnp.int32)
    allowed = band_mask + ident[None] > 0
    q_heads = own_q.reshape(q_rows, local_heads, HD)
    my_row = lax.dynamic_index_in_dim(allowed, place, 1, keepdims=False)
    k_piece = lax.all_gather(own_k, "seq", axis=0, tiled=True)
    v_piece = lax.all_gather(own_v, "seq", axis=0, tiled=True)
    count = k_piece.shape[0]
    band = jnp.arange(count) // kv_rows
    onehot = band[:, None] == bands[None, :]
    keymask = jnp.any(onehot[None] & my_row[:, None, :], axis=-1)
    top = jnp.full((local_heads, q_rows), -1e30, jnp.float32)
    k_heads = k_piece.reshape(count, local_heads, HD)
    v_heads = v_piece.reshape(count, local_heads, HD)
    scores = (
        jnp.einsum("qhd,khd->hqk", q_heads, k_heads, preferred_element_type=jnp.float32) * scale
    )
    scores = jnp.where(keymask[:, None, :], scores, -1e30)
    new_top = jnp.maximum(top, jnp.max(scores, axis=-1))
    expo = jnp.where(keymask[:, None, :], jnp.exp(scores - new_top[..., None]), 0.0)
    total = jnp.sum(expo, axis=-1)
    accum = jnp.einsum(
        "hqk,khd->hqd", expo.astype(jnp.bfloat16), v_heads, preferred_element_type=jnp.float32
    )
    top, total, accum = (new_top, total, accum)
    attn = accum / total[..., None]
    own_rows = jnp.transpose(attn, (1, 0, 2)).reshape(q_rows, local_heads * HD).astype(jnp.bfloat16)
    partner = swapped(own_rows, "cfg", 0)
    first_copy = lax.axis_index("cfg") == 0
    cond = jnp.where(first_copy, own_rows, partner).astype(jnp.float32)
    uncond = jnp.where(first_copy, partner, own_rows).astype(jnp.float32)
    guided = (uncond + guidance[0] * (cond - uncond)).astype(jnp.bfloat16)
    terms = jnp.dot(guided, out_weight, preferred_element_type=jnp.float32)
    return lax.psum_scatter(terms.astype(jnp.bfloat16), "head", scatter_dimension=1, tiled=True)


def shards(queries, *rest):
    seq = lax.axis_size("seq")
    heads = queries.shape[2] // HD
    sets = lax.axis_size("groups")
    pairs = lax.axis_size("cfg") == 2 and lax.axis_size("head") == 2 and sets > 1
    if pairs and heads % seq == 0 and seq % sets == 0 and seq & (seq - 1) == 0:
        return by_heads(queries, *rest)
    return by_rows(queries, *rest)


def solution(mesh):
    in_specs = (
        P("cfg", ("groups", "seq"), "head"),
        P("cfg", ("groups", "seq"), "head"),
        P("cfg", ("groups", "seq"), "head"),
        P(("groups", "head"), None, None),
        P("head", "cfg"),
        P(),
    )
    out_specs = P(("groups", "seq"), ("cfg", "head"))
    return jax.shard_map(shards, mesh=mesh, in_specs=in_specs, out_specs=out_specs, check_vma=False)
```

```python
import functools

import jax
import jax.numpy as jnp
from jax import lax
from jax.experimental import pallas as pl
from jax.experimental.pallas import tpu as pltpu
from jax.sharding import PartitionSpec as P

HD = 128
MESH = pl.DeviceIdType.MESH
LOG2E = 1.4426950408889634


def flipped(index, bits):
    out = index
    bit = 1
    while bit <= bits:
        if bits // bit % 2:
            out = out + bit - 2 * bit * lax.rem(lax.div(index, bit), 2)
        bit *= 2
    return out


def remote(src, dst, send, recv, device):
    copy = pltpu.make_async_remote_copy(
        src_ref=src, dst_ref=dst, send_sem=send, recv_sem=recv, device_id=device, device_id_type=MESH
    )
    copy.start()
    return copy


def kernel(
    n, hp, sets,
    q_ref, k_ref, v_ref, mask_ref, w_ref, g_ref, out_ref,
    q_buf, k_buf, v_buf, w_buf, att, other, guid, rows, acc,
    load_sem, w_sem, a_send, a_recv, x_send, x_recv, r_send, r_recv, f_send, f_recv,
    wx_send, wx_recv, wy_send, wy_recv,
):
    me = lax.axis_index("seq")
    core = lax.axis_index("cfg")
    side = lax.axis_index("head")
    group = lax.axis_index("groups")
    T = q_ref.shape[1]
    half = T // 2
    cols = out_ref.shape[1]
    share = n // sets
    tensors = ((k_ref, k_buf), (v_ref, v_buf), (q_ref, q_buf))
    sibling = {"cfg": 1 - core}
    across = {"head": 1 - side}
    groups = [{"groups": lax.rem(group + d, sets)} for d in range(1, sets)]

    barrier = pltpu.get_barrier_semaphore()
    for device in [{"seq": flipped(me, k)} for k in range(1, n)] + [sibling, across] + groups:
        pl.semaphore_signal(barrier, inc=1, device_id=device, device_id_type=MESH)

    loads = {}
    mine = pl.multiple_of(me * T, T)
    for j in range(hp):
        at = pl.multiple_of((me * hp + j) * HD, HD)
        for i, (ref, buf) in enumerate(tensors):
            loads[j, i] = pltpu.make_async_copy(
                ref.at[0, :, pl.ds(at, HD)], buf.at[j, pl.ds(mine, T), :], load_sem.at[j, i]
            )
            loads[j, i].start()
    w_loads = {}
    own_cols = pl.ds(pl.multiple_of(side * cols, cols), cols)
    for j in range(hp):
        for z in range(n):
            w_loads[j, z] = pltpu.make_async_copy(
                w_ref.at[pl.ds((z * hp + j) * HD, HD), own_cols], w_buf.at[0, j, pl.ds(z * HD, HD), :], w_sem.at[j, z]
            )
    pl.semaphore_wait(barrier, n - 1 + 2 + sets - 1)

    order = list(range(n - 1, 0, -1))
    a2a, across_w, swaps, backs, relays, group_w = {}, {}, {}, {}, {}, {}
    my_half = pl.ds(pl.multiple_of(core * half, half), half)
    own_at = pl.multiple_of(me * HD, HD)

    def exchange(j):
        for i, (ref, buf) in enumerate(tensors):
            for k in order:
                dest = flipped(me, k)
                at = pl.multiple_of((dest * hp + j) * HD, HD)
                a2a[j, k, i] = remote(
                    ref.at[0, :, pl.ds(at, HD)], buf.at[j, pl.ds(mine, T), :],
                    a_send.at[j, k - 1, i], a_recv.at[j, k - 1, i], {"seq": dest},
                )

    def place(slot, j, k):
        at = pl.multiple_of(flipped(me, k) * HD, HD)
        return rows.at[slot, j, my_half, pl.ds(at, HD)]

    def relay(kind, j, k, block, slot, device):
        relays[j, k, kind] = remote(
            block, place(slot, j, k), f_send.at[kind, j, k], f_recv.at[kind, j, k], device
        )

    def pass_on(j):
        for k in order:
            backs[j, k].wait_recv()
            relay(1, j, k, place(0, j, k), 1, across)
            relay(0, j, k, place(0, j, k), 0, sibling)

    def spread(j):
        for k in [0] + order:
            relays[j, k, 1].wait_recv()
            relay(2, j, k, place(1, j, k), 1, sibling)

    def project(j, slot):
        for k in range(n):
            for kind in ((0,), (2,))[slot]:
                relays[j, k, kind].wait_recv()
        term = jnp.dot(rows[slot, j], w_buf[slot, j], preferred_element_type=jnp.float32)
        if j + slot > 0:
            term = acc[...] + term
        if slot == 1 and j == hp - 1:
            out_ref[...] = term.astype(jnp.bfloat16)
        else:
            acc[...] = term

    their_cols = pl.ds(pl.multiple_of((1 - side) * cols, cols), cols)
    for j in range(hp):
        if j < 2:
            exchange(j)
        for i in range(share):
            z = group * share + i
            at = pl.multiple_of((z * hp + j) * HD, HD)
            across_w[j, i] = remote(
                w_ref.at[pl.ds(at, HD), their_cols],
                w_buf.at[1, j, pl.ds(pl.multiple_of(z * HD, HD), HD), :],
                wx_send.at[j, i], wx_recv.at[j, i], across,
            )
    for copy in w_loads.values():
        copy.start()

    scale = HD ** (-0.5) * LOG2E
    guidance = g_ref[0]
    first = core == 0

    def attend(j, k):
        head = me * hp + j
        t = flipped(me, k)
        q = q_buf[j, pl.ds(pl.multiple_of(t * T, T), T), :]
        s = lax.dot_general(q, k_buf[j], (((1,), (1,)), ((), ())), preferred_element_type=jnp.float32)
        pieces = []
        for b in range(n):
            listed = mask_ref[t, b, head] + (t == b).astype(jnp.int32)
            bias = jnp.where(listed > 0, 0.0, -1e30).astype(jnp.float32)
            pieces.append(s[:, b * T:(b + 1) * T] * scale + bias)
        s = jnp.concatenate(pieces, axis=1)
        top = jnp.max(s, axis=1, keepdims=True)
        expo = jnp.exp2(s - top)
        total = jnp.sum(expo, axis=1, keepdims=True)
        o = jnp.dot(expo.astype(jnp.bfloat16), v_buf[j], preferred_element_type=jnp.float32)
        o = (o * (1.0 / total)).astype(jnp.bfloat16)
        att[j, 0, t] = o[:half]
        att[j, 1, t] = o[half:]
        swaps[j, k] = remote(att.at[j, 1 - core, t], other.at[j, t], x_send.at[j, k], x_recv.at[j, k], sibling)

    def guide(j, k):
        t = flipped(me, k)
        swaps[j, k].wait_recv()
        own = att[j, core, t].astype(jnp.float32)
        oth = other[j, t].astype(jnp.float32)
        cond = jnp.where(first, own, oth)
        uncond = jnp.where(first, oth, own)
        guided = (uncond + guidance * (cond - uncond)).astype(jnp.bfloat16)
        guid[j, t] = guided
        if k == 0:
            rows[0, j, my_half, pl.ds(own_at, HD)] = guided
            relay(1, j, 0, guid.at[j, t], 1, across)
            relay(0, j, 0, guid.at[j, t], 0, sibling)
        else:
            backs[j, k] = remote(
                guid.at[j, t], rows.at[0, j, my_half, pl.ds(own_at, HD)],
                r_send.at[j, k - 1], r_recv.at[j, k - 1], {"seq": t},
            )

    for j in range(hp):
        for i in range(share):
            across_w[j, i].wait_recv()
            z = group * share + i
            block = w_buf.at[1, j, pl.ds(pl.multiple_of(z * HD, HD), HD), :]
            for d, device in enumerate(groups):
                group_w[d, j, i] = remote(block, block, wy_send.at[d, j, i], wy_recv.at[d, j, i], device)
        for i in range(3):
            loads[j, i].wait()
        for i in range(2):
            for k in order:
                a2a[j, k, i].wait_recv()
        before = None
        for k in [0] + order:
            if k > 0:
                a2a[j, k, 2].wait_recv()
            attend(j, k)
            if before is not None:
                guide(j, before)
            before = k
        guide(j, before)
        if j + 2 < hp:
            exchange(j + 2)
        if j > 0:
            pass_on(j - 1)
        if j > 1:
            spread(j - 2)

    for copy in w_loads.values():
        copy.wait()
    for copy in group_w.values():
        copy.wait_recv()
    for j in range(hp - 2):
        project(j, 0)
        project(j, 1)
    if hp > 1:
        spread(hp - 2)
    pass_on(hp - 1)
    if hp > 1:
        project(hp - 2, 0)
        project(hp - 2, 1)
    spread(hp - 1)
    project(hp - 1, 0)
    project(hp - 1, 1)
    for copies in (a2a, across_w, swaps, backs, relays, group_w):
        for copy in copies.values():
            copy.wait_send()


def by_heads(queries, keys, values, band_mask, out_weight, guidance):
    n = lax.axis_size("seq")
    sides = lax.axis_size("head")
    sets = lax.axis_size("groups")
    T, local = queries.shape[1], queries.shape[2]
    hp = local // HD // n
    cols = out_weight.shape[1] // sides
    half = T // 2
    share = n // sets
    bf = jnp.bfloat16
    any_spec = pl.BlockSpec(memory_space=pl.ANY)
    smem = pl.BlockSpec(memory_space=pltpu.SMEM)
    dma = pltpu.SemaphoreType.DMA
    return pl.pallas_call(
        functools.partial(kernel, n, hp, sets),
        out_shape=jax.ShapeDtypeStruct((T, cols), bf),
        in_specs=[any_spec, any_spec, any_spec, smem, any_spec, smem],
        out_specs=pl.BlockSpec(memory_space=pltpu.VMEM),
        scratch_shapes=[
            pltpu.VMEM((hp, n * T, HD), bf),
            pltpu.VMEM((hp, n * T, HD), bf),
            pltpu.VMEM((hp, n * T, HD), bf),
            pltpu.VMEM((sides, hp, n * HD, cols), bf),
            pltpu.VMEM((hp, 2, n, half, HD), bf),
            pltpu.VMEM((hp, n, half, HD), bf),
            pltpu.VMEM((hp, n, half, HD), bf),
            pltpu.VMEM((sides, hp, T, n * HD), bf),
            pltpu.VMEM((T, cols), jnp.float32),
            dma((hp, 3)), dma((hp, n)),
            dma((hp, n - 1, 3)), dma((hp, n - 1, 3)),
            dma((hp, n)), dma((hp, n)),
            dma((hp, n - 1)), dma((hp, n - 1)),
            dma((3, hp, n)), dma((3, hp, n)),
            dma((hp, share)), dma((hp, share)),
            dma((sets - 1, hp, share)), dma((sets - 1, hp, share)),
        ],
        compiler_params=pltpu.CompilerParams(
            collective_id=0, has_side_effects=True, vmem_limit_bytes=60 * 1024 * 1024
        ),
        name="by_heads",
    )(queries, keys, values, jnp.transpose(band_mask, (1, 2, 0)), out_weight, guidance)


def swapped(array, axis, bit):
    return lax.ppermute(array, axis, [(i, i ^ 1 << bit) for i in range(lax.axis_size(axis))])


def by_rows(queries, keys, values, band_mask, out_weight, guidance):
    own_q = queries[0]
    own_k = keys[0]
    own_v = values[0]
    q_rows = own_q.shape[0]
    kv_rows = own_k.shape[0]
    local_heads = own_q.shape[1] // HD
    tiles = lax.axis_size("seq")
    place = lax.axis_index("seq")
    scale = HD ** (-0.5)
    bands = jnp.arange(tiles)
    ident = (bands[:, None] == bands[None, :]).astype(jnp.int32)
    allowed = band_mask + ident[None] > 0
    q_heads = own_q.reshape(q_rows, local_heads, HD)
    my_row = lax.dynamic_index_in_dim(allowed, place, 1, keepdims=False)
    k_piece = lax.all_gather(own_k, "seq", axis=0, tiled=True)
    v_piece = lax.all_gather(own_v, "seq", axis=0, tiled=True)
    count = k_piece.shape[0]
    band = jnp.arange(count) // kv_rows
    onehot = band[:, None] == bands[None, :]
    keymask = jnp.any(onehot[None] & my_row[:, None, :], axis=-1)
    top = jnp.full((local_heads, q_rows), -1e30, jnp.float32)
    k_heads = k_piece.reshape(count, local_heads, HD)
    v_heads = v_piece.reshape(count, local_heads, HD)
    scores = (
        jnp.einsum("qhd,khd->hqk", q_heads, k_heads, preferred_element_type=jnp.float32) * scale
    )
    scores = jnp.where(keymask[:, None, :], scores, -1e30)
    new_top = jnp.maximum(top, jnp.max(scores, axis=-1))
    expo = jnp.where(keymask[:, None, :], jnp.exp(scores - new_top[..., None]), 0.0)
    total = jnp.sum(expo, axis=-1)
    accum = jnp.einsum(
        "hqk,khd->hqd", expo.astype(jnp.bfloat16), v_heads, preferred_element_type=jnp.float32
    )
    top, total, accum = (new_top, total, accum)
    attn = accum / total[..., None]
    own_rows = jnp.transpose(attn, (1, 0, 2)).reshape(q_rows, local_heads * HD).astype(jnp.bfloat16)
    partner = swapped(own_rows, "cfg", 0)
    first_copy = lax.axis_index("cfg") == 0
    cond = jnp.where(first_copy, own_rows, partner).astype(jnp.float32)
    uncond = jnp.where(first_copy, partner, own_rows).astype(jnp.float32)
    guided = (uncond + guidance[0] * (cond - uncond)).astype(jnp.bfloat16)
    terms = jnp.dot(guided, out_weight, preferred_element_type=jnp.float32)
    return lax.psum_scatter(terms.astype(jnp.bfloat16), "head", scatter_dimension=1, tiled=True)


def shards(queries, *rest):
    seq = lax.axis_size("seq")
    heads = queries.shape[2] // HD
    sets = lax.axis_size("groups")
    pairs = lax.axis_size("cfg") == 2 and lax.axis_size("head") == 2 and sets > 1
    if pairs and heads % seq == 0 and seq % sets == 0 and seq & (seq - 1) == 0:
        return by_heads(queries, *rest)
    return by_rows(queries, *rest)


def solution(mesh):
    in_specs = (
        P("cfg", ("groups", "seq"), "head"),
        P("cfg", ("groups", "seq"), "head"),
        P("cfg", ("groups", "seq"), "head"),
        P(("groups", "head"), None, None),
        P("head", "cfg"),
        P(),
    )
    out_specs = P(("groups", "seq"), ("cfg", "head"))
    return jax.shard_map(shards, mesh=mesh, in_specs=in_specs, out_specs=out_specs, check_vma=False)
```

```python
import functools

import jax
import jax.numpy as jnp
from jax import lax
from jax.experimental import pallas as pl
from jax.experimental.pallas import tpu as pltpu
from jax.sharding import PartitionSpec as P

HD = 128
MESH = pl.DeviceIdType.MESH
LOG2E = 1.4426950408889634


def flipped(index, bits):
    out = index
    bit = 1
    while bit <= bits:
        if bits // bit % 2:
            out = out + bit - 2 * bit * lax.rem(lax.div(index, bit), 2)
        bit *= 2
    return out


def remote(src, dst, send, recv, device):
    copy = pltpu.make_async_remote_copy(
        src_ref=src, dst_ref=dst, send_sem=send, recv_sem=recv, device_id=device, device_id_type=MESH
    )
    copy.start()
    return copy


def kernel(
    n, hp, sets,
    q_ref, k_ref, v_ref, mask_ref, w_ref, g_ref, out_ref,
    q_buf, k_buf, v_buf, w_buf, att, other, guid, rows, acc,
    load_sem, w_sem, a_send, a_recv, x_send, x_recv, r_send, r_recv, f_send, f_recv,
    wx_send, wx_recv, wy_send, wy_recv,
):
    me = lax.axis_index("seq")
    core = lax.axis_index("cfg")
    side = lax.axis_index("head")
    group = lax.axis_index("groups")
    T = q_ref.shape[1]
    half = T // 2
    cols = out_ref.shape[1]
    share = n // sets
    tensors = ((q_ref, q_buf), (k_ref, k_buf), (v_ref, v_buf))
    sibling = {"cfg": 1 - core}
    across = {"head": 1 - side}
    facing = {"head": 1 - side, "cfg": 1 - core}
    groups = [{"groups": lax.rem(group + d, sets)} for d in range(1, sets)]

    barrier = pltpu.get_barrier_semaphore()
    for device in [{"seq": flipped(me, k)} for k in range(1, n)] + [sibling, across, facing] + groups:
        pl.semaphore_signal(barrier, inc=1, device_id=device, device_id_type=MESH)

    loads = {}
    mine = pl.multiple_of(me * T, T)
    for j in range(hp):
        at = pl.multiple_of((me * hp + j) * HD, HD)
        for i, (ref, buf) in enumerate(tensors):
            loads[j, i] = pltpu.make_async_copy(
                ref.at[0, :, pl.ds(at, HD)], buf.at[j, pl.ds(mine, T), :], load_sem.at[j, i]
            )
            loads[j, i].start()
    w_loads = {}
    own_cols = pl.ds(pl.multiple_of(side * cols, cols), cols)
    for j in range(hp):
        for z in range(n):
            w_loads[j, z] = pltpu.make_async_copy(
                w_ref.at[pl.ds((z * hp + j) * HD, HD), own_cols], w_buf.at[0, j, pl.ds(z * HD, HD), :], w_sem.at[j, z]
            )
    pl.semaphore_wait(barrier, n - 1 + 3 + sets - 1)

    a2a = {}
    across_w = {}
    their_cols = pl.ds(pl.multiple_of((1 - side) * cols, cols), cols)
    def exchange(j):
        for k in range(n - 1, 0, -1):
            dest = flipped(me, k)
            at = pl.multiple_of((dest * hp + j) * HD, HD)
            for i, (ref, buf) in enumerate(tensors):
                a2a[j, k, i] = remote(
                    ref.at[0, :, pl.ds(at, HD)], buf.at[j, pl.ds(mine, T), :],
                    a_send.at[j, k - 1, i], a_recv.at[j, k - 1, i], {"seq": dest},
                )

    for j in range(hp):
        if j < 2:
            exchange(j)
        for i in range(share):
            z = group * share + i
            at = pl.multiple_of((z * hp + j) * HD, HD)
            across_w[j, i] = remote(
                w_ref.at[pl.ds(at, HD), their_cols],
                w_buf.at[1, j, pl.ds(pl.multiple_of(z * HD, HD), HD), :],
                wx_send.at[j, i], wx_recv.at[j, i], across,
            )
    for copy in w_loads.values():
        copy.start()

    scale = HD ** (-0.5) * LOG2E
    guidance = g_ref[0]
    first = core == 0
    my_half = pl.ds(pl.multiple_of(core * half, half), half)
    swaps, backs, relays, group_w = {}, {}, {}, {}

    def pass_on(j, src, block, z, at):
        for i, (slot, device) in enumerate(((0, sibling), (1, across), (1, facing))):
            relays[j, src, i] = remote(
                block, rows.at[slot, j, my_half, pl.ds(at, HD)], f_send.at[i, j, src], f_recv.at[i, j, src], device
            )

    def forward(j):
        for k in range(1, n):
            backs[j, k].wait_recv()
            z = flipped(me, k)
            at = pl.multiple_of(z * HD, HD)
            pass_on(j, k, rows.at[0, j, my_half, pl.ds(at, HD)], z, at)

    for j in range(hp):
        for i in range(share):
            across_w[j, i].wait_recv()
            z = group * share + i
            block = w_buf.at[1, j, pl.ds(pl.multiple_of(z * HD, HD), HD), :]
            for d, device in enumerate(groups):
                group_w[d, j, i] = remote(block, block, wy_send.at[d, j, i], wy_recv.at[d, j, i], device)
        for i in range(3):
            loads[j, i].wait()
            for k in range(1, n):
                a2a[j, k, i].wait_recv()
        head = me * hp + j
        for t in range(n):
            q = q_buf[j, t * T:(t + 1) * T, :]
            s = lax.dot_general(q, k_buf[j], (((1,), (1,)), ((), ())), preferred_element_type=jnp.float32)
            pieces = []
            for b in range(n):
                piece = s[:, b * T:(b + 1) * T] * scale
                if b != t:
                    piece = piece + jnp.where(mask_ref[t, b, head] > 0, 0.0, -1e30).astype(jnp.float32)
                pieces.append(piece)
            s = jnp.concatenate(pieces, axis=1)
            top = jnp.max(s, axis=1, keepdims=True)
            expo = jnp.exp2(s - top)
            total = jnp.sum(expo, axis=1, keepdims=True)
            o = jnp.dot(expo.astype(jnp.bfloat16), v_buf[j], preferred_element_type=jnp.float32)
            o = (o * (1.0 / total)).astype(jnp.bfloat16)
            att[j, 0, t] = o[:half]
            att[j, 1, t] = o[half:]
        swaps[j] = remote(att.at[j, 1 - core], other.at[j], x_send.at[j], x_recv.at[j], sibling)
        swaps[j].wait_recv()
        own = att[j, core].astype(jnp.float32)
        oth = other[j].astype(jnp.float32)
        cond = jnp.where(first, own, oth)
        uncond = jnp.where(first, oth, own)
        guid[j] = (uncond + guidance * (cond - uncond)).astype(jnp.bfloat16)
        own_at = pl.multiple_of(me * HD, HD)
        for k in range(n - 1, 0, -1):
            dest = flipped(me, k)
            backs[j, k] = remote(
                guid.at[j, dest], rows.at[0, j, my_half, pl.ds(own_at, HD)],
                r_send.at[j, k - 1], r_recv.at[j, k - 1], {"seq": dest},
            )
        pass_on(j, 0, guid.at[j, me], me, own_at)
        rows[0, j, my_half, pl.ds(own_at, HD)] = guid[j, me]
        if j + 2 < hp:
            exchange(j + 2)
        if 0 < j < hp - 1:
            forward(j - 1)

    for j in range(max(hp - 2, 0), hp):
        forward(j)

    for copy in w_loads.values():
        copy.wait()
    for copy in group_w.values():
        copy.wait_recv()
    for j in range(hp):
        for slot, kinds in ((0, (0,)), (1, (1, 2))):
            for k in range(n):
                for i in kinds:
                    relays[j, k, i].wait_recv()
            term = jnp.dot(rows[slot, j], w_buf[slot, j], preferred_element_type=jnp.float32)
            if j + slot > 0:
                term = acc[...] + term
            if slot == 1 and j == hp - 1:
                out_ref[...] = term.astype(jnp.bfloat16)
            else:
                acc[...] = term
    for copies in (a2a, across_w, swaps, backs, relays, group_w):
        for copy in copies.values():
            copy.wait_send()


def by_heads(queries, keys, values, band_mask, out_weight, guidance):
    n = lax.axis_size("seq")
    sides = lax.axis_size("head")
    sets = lax.axis_size("groups")
    T, local = queries.shape[1], queries.shape[2]
    hp = local // HD // n
    cols = out_weight.shape[1] // sides
    half = T // 2
    share = n // sets
    bf = jnp.bfloat16
    any_spec = pl.BlockSpec(memory_space=pl.ANY)
    smem = pl.BlockSpec(memory_space=pltpu.SMEM)
    dma = pltpu.SemaphoreType.DMA
    return pl.pallas_call(
        functools.partial(kernel, n, hp, sets),
        out_shape=jax.ShapeDtypeStruct((T, cols), bf),
        in_specs=[any_spec, any_spec, any_spec, smem, any_spec, smem],
        out_specs=pl.BlockSpec(memory_space=pltpu.VMEM),
        scratch_shapes=[
            pltpu.VMEM((hp, n * T, HD), bf),
            pltpu.VMEM((hp, n * T, HD), bf),
            pltpu.VMEM((hp, n * T, HD), bf),
            pltpu.VMEM((sides, hp, n * HD, cols), bf),
            pltpu.VMEM((hp, 2, n, half, HD), bf),
            pltpu.VMEM((hp, n, half, HD), bf),
            pltpu.VMEM((hp, n, half, HD), bf),
            pltpu.VMEM((sides, hp, T, n * HD), bf),
            pltpu.VMEM((T, cols), jnp.float32),
            dma((hp, 3)), dma((hp, n)),
            dma((hp, n - 1, 3)), dma((hp, n - 1, 3)),
            dma((hp,)), dma((hp,)),
            dma((hp, n - 1)), dma((hp, n - 1)),
            dma((3, hp, n)), dma((3, hp, n)),
            dma((hp, share)), dma((hp, share)),
            dma((sets - 1, hp, share)), dma((sets - 1, hp, share)),
        ],
        compiler_params=pltpu.CompilerParams(
            collective_id=0, has_side_effects=True, vmem_limit_bytes=60 * 1024 * 1024
        ),
        name="by_heads",
    )(queries, keys, values, jnp.transpose(band_mask, (1, 2, 0)), out_weight, guidance)


def swapped(array, axis, bit):
    return lax.ppermute(array, axis, [(i, i ^ 1 << bit) for i in range(lax.axis_size(axis))])


def by_rows(queries, keys, values, band_mask, out_weight, guidance):
    own_q = queries[0]
    own_k = keys[0]
    own_v = values[0]
    q_rows = own_q.shape[0]
    kv_rows = own_k.shape[0]
    local_heads = own_q.shape[1] // HD
    tiles = lax.axis_size("seq")
    place = lax.axis_index("seq")
    scale = HD ** (-0.5)
    bands = jnp.arange(tiles)
    ident = (bands[:, None] == bands[None, :]).astype(jnp.int32)
    allowed = band_mask + ident[None] > 0
    q_heads = own_q.reshape(q_rows, local_heads, HD)
    my_row = lax.dynamic_index_in_dim(allowed, place, 1, keepdims=False)
    k_piece = lax.all_gather(own_k, "seq", axis=0, tiled=True)
    v_piece = lax.all_gather(own_v, "seq", axis=0, tiled=True)
    count = k_piece.shape[0]
    band = jnp.arange(count) // kv_rows
    onehot = band[:, None] == bands[None, :]
    keymask = jnp.any(onehot[None] & my_row[:, None, :], axis=-1)
    top = jnp.full((local_heads, q_rows), -1e30, jnp.float32)
    k_heads = k_piece.reshape(count, local_heads, HD)
    v_heads = v_piece.reshape(count, local_heads, HD)
    scores = (
        jnp.einsum("qhd,khd->hqk", q_heads, k_heads, preferred_element_type=jnp.float32) * scale
    )
    scores = jnp.where(keymask[:, None, :], scores, -1e30)
    new_top = jnp.maximum(top, jnp.max(scores, axis=-1))
    expo = jnp.where(keymask[:, None, :], jnp.exp(scores - new_top[..., None]), 0.0)
    total = jnp.sum(expo, axis=-1)
    accum = jnp.einsum(
        "hqk,khd->hqd", expo.astype(jnp.bfloat16), v_heads, preferred_element_type=jnp.float32
    )
    top, total, accum = (new_top, total, accum)
    attn = accum / total[..., None]
    own_rows = jnp.transpose(attn, (1, 0, 2)).reshape(q_rows, local_heads * HD).astype(jnp.bfloat16)
    partner = swapped(own_rows, "cfg", 0)
    first_copy = lax.axis_index("cfg") == 0
    cond = jnp.where(first_copy, own_rows, partner).astype(jnp.float32)
    uncond = jnp.where(first_copy, partner, own_rows).astype(jnp.float32)
    guided = (uncond + guidance[0] * (cond - uncond)).astype(jnp.bfloat16)
    terms = jnp.dot(guided, out_weight, preferred_element_type=jnp.float32)
    return lax.psum_scatter(terms.astype(jnp.bfloat16), "head", scatter_dimension=1, tiled=True)


def shards(queries, *rest):
    seq = lax.axis_size("seq")
    heads = queries.shape[2] // HD
    sets = lax.axis_size("groups")
    pairs = lax.axis_size("cfg") == 2 and lax.axis_size("head") == 2 and sets > 1
    if pairs and heads % seq == 0 and seq % sets == 0 and seq & (seq - 1) == 0:
        return by_heads(queries, *rest)
    return by_rows(queries, *rest)


def solution(mesh):
    in_specs = (
        P("cfg", ("groups", "seq"), "head"),
        P("cfg", ("groups", "seq"), "head"),
        P("cfg", ("groups", "seq"), "head"),
        P(("groups", "head"), None, None),
        P("head", "cfg"),
        P(),
    )
    out_specs = P(("groups", "seq"), ("cfg", "head"))
    return jax.shard_map(shards, mesh=mesh, in_specs=in_specs, out_specs=out_specs, check_vma=False)
```
